32 devices in a mesh: member: 2 (over y), lon: 8 (over z, x), lat: 2 (over core).
Axes of the slice: x: 2, y: 2, z: 4, core: 2. Of those that a mesh axis runs over, the one named last changes fastest.
Arguments:
- fields: bfloat16 [1280, 32, 128], P('member', 'lat', 'lon'), parts along dimension 0, may hold values from -6 to 6
- support_rows: int32 [7, 32, 16], replicated, may hold values from -1 to 1
- support_lons: int32 [7, 32, 16], replicated, may hold values from -64 to 64, as said below
- support_weights: float32 [7, 32, 16], replicated, may hold values from -1.5 to 1.5
- mix_weight: bfloat16 [7, 640, 640], replicated, may hold values from -0.09375 to 0.09375
- norm_gain: float32 [640], replicated, may hold values from 0.1 to 1.9
- up_weight: bfloat16 [640, 1280], replicated, may hold values from -0.25 to 0.25
- down_weight: bfloat16 [1280, 640], replicated, may hold values from -0.15625 to 0.15625
Outputs:
- output: bfloat16 [1280, 32, 128], P('member', 'lat', 'lon'), parts along dimension 0
The draws below stay inside these ranges and needn't reach their ends.
There are 2 independent parts, one for each index of `member`. The reference program is written for one: setup_inputs(seed, part) draws one part's arguments, and reference() takes and returns one part's arrays. A program takes and returns all parts, laid end to end along the dimension named above; an argument that names none is the same for every part. Nothing has to cross between parts.
Inputs may be any that keep to these rules, and one draw needn't show every extreme that they name: `support_lons`: at output row i every offset lies within plus or minus min(64, 4 * 32 // min(i + 1, 32 - i)); in every basis filter the first pole row has an entry at -(64) and the last pole row one at 64.
All inputs are finite; a program needn't handle non-finite values.
Results may differ from the reference program's by a relative error of at most 0.0095.
Values may be sent and summed in bfloat16 or wider, within the bound.
A program may use at most 128 MiB of HBM per device.

```python
import math
import jax
import jax.numpy as jnp
from jax import lax

C = 640
HID = 1280
K = 7
S = 16
NLAT = 32
NLON = 128


def draw_support_rows(key, part):
    return jax.random.randint(key, (K, NLAT, S), -1, 2, dtype=jnp.int32)


def draw_support_lons(key, part):
    row_index = lax.broadcasted_iota(jnp.int32, (K, NLAT, S), 1)
    slot_index = lax.broadcasted_iota(jnp.int32, (K, NLAT, S), 2)
    nearest = jnp.minimum(row_index + 1, NLAT - row_index)
    half_reach = jnp.minimum(NLON // 2, 4 * NLAT // nearest)
    random_bits = jax.random.randint(key, (K, NLAT, S), 0, 2 ** 30, dtype=jnp.int32)
    offset = jnp.mod(random_bits, 2 * half_reach + 1) - half_reach
    offset = jnp.where((row_index == 0) & (slot_index == 0), -(NLON // 2), offset)
    offset = jnp.where((row_index == NLAT - 1) & (slot_index == 0), NLON // 2, offset)
    return offset.astype(jnp.int32)


def block_levels(rng, extent, shards, smallest, largest):
    loudness, own = 1.0, jax.random.fold_in(rng, 6)
    for dim, shards_of in shards:
        heights = jnp.exp(jax.random.uniform(jax.random.fold_in(own, dim), (shards_of,), jnp.float32, smallest / len(shards), largest / len(shards)))
        loudness = loudness * jnp.repeat(heights, extent[dim] // shards_of).reshape([-1 if axis == dim else 1 for axis in range(len(extent))])
    return loudness


def bell_draw(key, shape, width, reach, split=(), kind=jnp.bfloat16):
    drawn = jax.random.normal(key, shape, jnp.float32) * width
    if len(split) > 0:
        drawn = block_levels(key, shape, split, -0.22, 0.18) * drawn
    return jnp.clip(drawn, min=-reach, max=reach).astype(kind)


def setup_inputs(seed: int = 0, part: int = 0) -> dict:
    seeds = jax.random.split(jax.random.key(seed), 9)
    part_keys = jax.random.split(jax.random.fold_in(seeds[8], part), 9)
    return {
        "fields": bell_draw(part_keys[0], (C, NLAT, NLON), 1.0, 6.0, ((1, 2), (2, 8))),
        "support_rows": draw_support_rows(jax.random.fold_in(seeds[8], 71), part),
        "support_lons": draw_support_lons(jax.random.fold_in(seeds[8], 71), part),
        "support_weights": bell_draw(seeds[3], (K, NLAT, S), 0.25, 1.5, (), jnp.float32),
        "mix_weight": bell_draw(seeds[4], (K, C, C), (K * C) ** -0.5, 0.09375),
        "norm_gain": jnp.clip(1.0 + 0.18 * jax.random.normal(seeds[5], (C,), jnp.float32), 0.1, 1.9),
        "up_weight": bell_draw(seeds[6], (C, HID), C ** -0.5, 0.25),
        "down_weight": bell_draw(seeds[7], (HID, C), HID ** -0.5, 0.15625),
    }


full_turn = 2.0 * math.pi
norm_eps = 1e-05

def round_half(values):
    return lax.optimization_barrier(values.astype(jnp.bfloat16)).astype(jnp.float32)

def reference(fields, support_rows, support_lons, support_weights, mix_weight, norm_gain, up_weight, down_weight):
    lon_total = NLON
    lon_half = lon_total // 2
    frequency = jnp.arange(lon_half + 1, dtype=jnp.int32)
    spectrum = jnp.fft.rfft(fields.astype(jnp.float32), axis=2)
    cos_part = jnp.pad(round_half(jnp.real(spectrum).astype(jnp.float32)), ((0, 0), (1, 1), (0, 0)))
    sin_part = jnp.pad(round_half((-jnp.imag(spectrum)).astype(jnp.float32)), ((0, 0), (1, 1), (0, 0)))

    def basis_term(running, basis_index):
        row_offsets = support_rows[basis_index]
        lon_offsets = support_lons[basis_index]
        weights = support_weights[basis_index]
        turns = jnp.mod(lon_offsets[:, :, None] * frequency[None, None, :], lon_total).astype(jnp.int32)
        phase_angle = turns.astype(jnp.float32) * (full_turn / lon_total)
        cos_table = jnp.cos(phase_angle)
        sin_table = jnp.sin(phase_angle)
        spec_cos = jnp.zeros((C, NLAT, lon_half + 1), jnp.float32)
        spec_sin = jnp.zeros((C, NLAT, lon_half + 1), jnp.float32)
        for offset in (-1, 0, 1):
            picked = jnp.where(row_offsets == offset, weights, jnp.zeros_like(weights))
            filter_cos = jnp.einsum('is,isf->if', picked, cos_table, precision=lax.Precision.HIGHEST)
            filter_sin = jnp.einsum('is,isf->if', picked, sin_table, precision=lax.Precision.HIGHEST)
            field_cos = cos_part[:, 1 + offset:1 + offset + NLAT]
            field_sin = sin_part[:, 1 + offset:1 + offset + NLAT]
            spec_cos = spec_cos + field_cos * filter_cos + field_sin * filter_sin
            spec_sin = spec_sin + field_sin * filter_cos - field_cos * filter_sin
        weight_k = mix_weight[basis_index]
        run_cos = running[0] + lax.dot_general(weight_k, spec_cos.astype(jnp.bfloat16).reshape(C, -1), (((0,), (0,)), ((), ())), preferred_element_type=jnp.float32)
        run_sin = running[1] + lax.dot_general(weight_k, spec_sin.astype(jnp.bfloat16).reshape(C, -1), (((0,), (0,)), ((), ())), preferred_element_type=jnp.float32)
        return ((run_cos, run_sin), None)
    start = jnp.zeros((C, NLAT * (lon_half + 1)), jnp.float32)
    mixed_parts, _ = lax.scan(basis_term, (start, start), jnp.arange(K, dtype=jnp.int32))
    mixed_cos = mixed_parts[0].reshape(C, NLAT, lon_half + 1)
    mixed_sin = mixed_parts[1].reshape(C, NLAT, lon_half + 1)
    mixed = jnp.fft.irfft(lax.complex(mixed_cos, -mixed_sin), n=lon_total, axis=2).astype(jnp.float32)
    latent = fields.reshape(C, NLAT * NLON).astype(jnp.float32) + mixed.reshape(C, NLAT * NLON)
    row_mean = lax.optimization_barrier(jnp.mean(latent, axis=0))
    variance = lax.optimization_barrier(jnp.mean(jnp.square(latent - row_mean), axis=0))
    normed = ((latent - row_mean) * lax.rsqrt(variance + norm_eps) * norm_gain[:, None]).astype(jnp.bfloat16)
    hidden = jax.nn.gelu(lax.dot_general(up_weight, normed, (((0,), (0,)), ((), ())), preferred_element_type=jnp.float32), approximate=False).astype(jnp.bfloat16)
    output = latent + lax.dot_general(down_weight, hidden, (((0,), (0,)), ((), ())), preferred_element_type=jnp.float32)
    return output.astype(jnp.bfloat16).reshape(C, NLAT, NLON)
```

```python
import functools
import math

import jax
import jax.numpy as jnp
from jax import lax
from jax.experimental import pallas as pl
from jax.experimental.pallas import tpu as pltpu
from jax.sharding import PartitionSpec as P

norm_eps = 1e-05
MESH = pl.DeviceIdType.MESH


def plan_copies(lon_count, lat_count, rows, cols):
    lon_total, row_total = lon_count * cols, lat_count * rows

    def distance(row):
        nearest = min(row + 1, row_total - row)
        reach = min(lon_total // 2, 4 * row_total // nearest)
        return min(-(-reach // cols), lon_count // 2)

    need = [distance(max(p - 1, 0)) for p in range(rows)]
    split = rows // 2 - 1
    early, late = [], []
    for delta in range(-(lon_count // 2) + 1, lon_count // 2 + 1):
        if delta == 0:
            continue
        count = sum(1 for d in need if d >= abs(delta))
        if count > split:
            early.append(("block", delta, split, count))
        if min(count, split) > 0:
            late.append(("block", delta, 0, min(count, split)))
    edge = 0
    for boundary in range(1, lat_count):
        edge = max(edge, distance(boundary * rows - 1), distance(boundary * rows))
    halo = []
    if lat_count > 1:
        for delta in range(-(lon_count // 2) + 1, lon_count // 2 + 1):
            if abs(delta) <= edge:
                halo.append(("down", delta, 0, 1))
                halo.append(("up", delta, 0, 1))
    late.sort(key=lambda item: -abs(item[1]))
    return halo + early, late


def block_kernel(
    lon_count,
    lat_count,
    early,
    late,
    x_ref,
    rows_ref,
    lons_ref,
    weights_ref,
    gain_ref,
    mix_hbm,
    up_hbm,
    down_hbm,
    out_ref,
    window,
    filters,
    product,
    mix_ref,
    up_ref,
    down_ref,
    send_sem,
    recv_sem,
    load_sem,
):
    rows, cols, channels = x_ref.shape
    bases = mix_ref.shape[0] // channels
    entries = rows_ref.shape[2]
    lon_total = lon_count * cols
    middle = lon_count // 2
    half = rows // 2
    me, lat = lax.axis_index("lon"), lax.axis_index("lat")
    north = 2 * lat < lat_count
    has_low, has_high = lat > 0, lat < lat_count - 1

    loads = [
        pltpu.make_async_copy(mix_hbm, mix_ref, load_sem.at[0]),
        pltpu.make_async_copy(up_hbm, up_ref, load_sem.at[1]),
        pltpu.make_async_copy(down_hbm, down_ref, load_sem.at[2]),
    ]
    for load in loads:
        load.start()

    window[...] = jnp.zeros_like(window)
    window[1 : rows + 1, middle * cols : (middle + 1) * cols, :] = x_ref[...]

    barrier = pltpu.get_barrier_semaphore()
    halo_deltas = [item[1] for item in early if item[0] == "down"]
    for delta in range(1, lon_count):
        pl.semaphore_signal(
            barrier, inc=1, device_id={"lon": lax.rem(me + delta, lon_count)}, device_id_type=MESH
        )
    for present, other in ((has_low, lat - 1), (has_high, lat + 1)):

        @pl.when(present)
        def _():
            for delta in halo_deltas:
                target = lax.rem(me + lon_count - delta, lon_count)
                pl.semaphore_signal(
                    barrier, inc=1, device_id={"lon": target, "lat": other}, device_id_type=MESH
                )

    sides = jnp.where(has_low, 1, 0) + jnp.where(has_high, 1, 0)
    pl.semaphore_wait(barrier, lon_count - 1 + sides * len(halo_deltas))

    def copy_of(index, item):
        kind, delta, first, last = item
        target = lax.rem(me + lon_count - delta, lon_count)
        slot = (delta + middle) % lon_count
        if kind == "block":
            start = jnp.where(north, first, rows - last)
            source = x_ref.at[pl.ds(start, last - first)]
            landing = window.at[pl.ds(start + 1, last - first), pl.ds(slot * cols, cols)]
            device = {"lon": target}
        elif kind == "down":
            source = x_ref.at[pl.ds(rows - 1, 1)]
            landing = window.at[pl.ds(0, 1), pl.ds(slot * cols, cols)]
            device = {"lon": target, "lat": jnp.minimum(lat + 1, lat_count - 1)}
        else:
            source = x_ref.at[pl.ds(0, 1)]
            landing = window.at[pl.ds(rows + 1, 1), pl.ds(slot * cols, cols)]
            device = {"lon": target, "lat": jnp.maximum(lat - 1, 0)}
        return pltpu.make_async_remote_copy(
            src_ref=source,
            dst_ref=landing,
            send_sem=send_sem.at[index],
            recv_sem=recv_sem.at[index],
            device_id=device,
            device_id_type=MESH,
        )

    copies = list(enumerate(early + late))

    def each(items, sending, action):
        for index, item in items:
            if item[0] == "block":
                action(copy_of(index, item))
            else:
                present = has_high if (item[0] == "down") == sending else has_low

                @pl.when(present)
                def _():
                    action(copy_of(index, item))

    each(copies, True, lambda copy: copy.start())

    first_row = pl.multiple_of(lat * rows, rows)
    lanes = lax.broadcasted_iota(jnp.int32, (rows, lon_total), 1)

    def build(k, carry):
        spot = lons_ref[k, pl.ds(first_row, rows), :] + middle * cols
        spot = jnp.where(spot >= lon_total, spot - lon_total, spot)
        row_offset = rows_ref[k, pl.ds(first_row, rows), :]
        weight = weights_ref[k, pl.ds(first_row, rows), :]
        picked = [jnp.where(row_offset == r, weight, 0.0) for r in (-1, 0, 1)]
        sums = [jnp.zeros((rows, lon_total), jnp.float32) for _ in range(3)]
        for s in range(entries):
            hit = spot[:, s : s + 1] == lanes
            for r in range(3):
                sums[r] = sums[r] + jnp.where(hit, picked[r][:, s : s + 1], 0.0)
        for r in range(3):
            for i in range(rows):
                line = jnp.broadcast_to(sums[r][i : i + 1, :], (cols, lon_total))
                turned = pltpu.roll(line, 0, 1, stride=1, stride_axis=0)
                filters[i, pl.ds(pl.multiple_of(k * cols, cols), cols),
                        r * lon_total : (r + 1) * lon_total] = turned.astype(jnp.bfloat16)
        return carry

    lax.fori_loop(0, bases, build, 0)

    def group(start):
        def filter_row(t, carry):
            i = start + t
            source = window[pl.ds(i, 3)].reshape(3 * lon_total, channels)
            filtered = jnp.dot(filters[i], source, preferred_element_type=jnp.float32)
            filtered = filtered.astype(jnp.bfloat16)
            at = pl.multiple_of(t * cols, cols)
            for k in range(bases):
                product[pl.ds(at, cols), k * channels : (k + 1) * channels] = filtered[
                    k * cols : (k + 1) * cols
                ]
            return carry

        lax.fori_loop(0, half, filter_row, 0)
        mixed = jnp.dot(product[...], mix_ref[...], preferred_element_type=jnp.float32)
        own = x_ref[pl.ds(start, half)].reshape(half * cols, channels)
        latent = own.astype(jnp.float32) + mixed
        mean = jnp.mean(latent, axis=1, keepdims=True)
        centred = latent - mean
        variance = jnp.mean(centred * centred, axis=1, keepdims=True)
        normed = (centred * lax.rsqrt(variance + norm_eps) * gain_ref[...]).astype(jnp.bfloat16)
        raised = jnp.dot(normed, up_ref[...], preferred_element_type=jnp.float32)
        hidden = 0.5 * raised * (1.0 + lax.erf(raised * math.sqrt(0.5)))
        lowered = jnp.dot(
            hidden.astype(jnp.bfloat16), down_ref[...], preferred_element_type=jnp.float32
        )
        result = (latent + lowered).astype(jnp.bfloat16)
        out_ref[pl.ds(start, half)] = result.reshape(half, cols, channels)

    each(copies[: len(early)], False, lambda copy: copy.wait_recv())
    loads[0].wait()
    loads[1].wait()
    loads[2].wait()
    group(jnp.where(north, half, 0))
    each(copies[len(early) :], False, lambda copy: copy.wait_recv())
    group(jnp.where(north, 0, half))
    each(copies, True, lambda copy: copy.wait_send())


def on_device(
    lon_count,
    lat_count,
    fields,
    support_rows,
    support_lons,
    support_weights,
    mix_weight,
    norm_gain,
    up_weight,
    down_weight,
):
    channels, rows, cols = fields.shape
    bases, hidden = mix_weight.shape[0], up_weight.shape[1]
    lon_total = lon_count * cols
    early, late = plan_copies(lon_count, lat_count, rows, cols)
    count = len(early) + len(late)
    in_vmem = pl.BlockSpec(memory_space=pltpu.VMEM)
    anywhere = pl.BlockSpec(memory_space=pl.ANY)
    result = pl.pallas_call(
        functools.partial(block_kernel, lon_count, lat_count, early, late),
        out_shape=jax.ShapeDtypeStruct((rows, cols, channels), jnp.bfloat16),
        in_specs=[in_vmem] * 5 + [anywhere] * 3,
        out_specs=in_vmem,
        scratch_shapes=[
            pltpu.VMEM((rows + 2, lon_total, channels), jnp.bfloat16),
            pltpu.VMEM((rows, bases * cols, 3 * lon_total), jnp.bfloat16),
            pltpu.VMEM((rows // 2 * cols, bases * channels), jnp.bfloat16),
            pltpu.VMEM((bases * channels, channels), jnp.bfloat16),
            pltpu.VMEM((channels, hidden), jnp.bfloat16),
            pltpu.VMEM((hidden, channels), jnp.bfloat16),
            pltpu.SemaphoreType.DMA((count,)),
            pltpu.SemaphoreType.DMA((count,)),
            pltpu.SemaphoreType.DMA((3,)),
        ],
        compiler_params=pltpu.CompilerParams(
            collective_id=0, has_side_effects=True, vmem_limit_bytes=56 * 1024 * 1024
        ),
    )(
        jnp.transpose(fields, (1, 2, 0)),
        support_rows,
        support_lons,
        support_weights,
        norm_gain.reshape(1, channels),
        mix_weight.reshape(bases * channels, channels),
        up_weight,
        down_weight,
    )
    return jnp.transpose(result, (2, 0, 1))


def solution(mesh):
    in_specs = (P("member", "lat", "lon"), P(), P(), P(), P(), P(), P(), P())
    out_specs = P("member", "lat", "lon")
    return jax.shard_map(
        functools.partial(on_device, mesh.shape["lon"], mesh.shape["lat"]),
        mesh=mesh,
        in_specs=in_specs,
        out_specs=out_specs,
        check_vma=False,
    )
```

```python
import functools
import math

import jax
import jax.numpy as jnp
from jax import lax
from jax.experimental import pallas as pl
from jax.experimental.pallas import tpu as pltpu
from jax.sharding import PartitionSpec as P

norm_eps = 1e-05
MESH = pl.DeviceIdType.MESH


def plan_copies(lon_count, lat_count, rows, cols):
    lon_total, row_total = lon_count * cols, lat_count * rows

    def distance(row):
        nearest = min(row + 1, row_total - row)
        reach = min(lon_total // 2, 4 * row_total // nearest)
        return min(-(-reach // cols), lon_count // 2)

    need = [distance(max(p - 1, 0)) for p in range(rows)]
    deltas = [d for d in range(1 - lon_count // 2, lon_count // 2 + 1) if d != 0]
    counts = {delta: sum(1 for d in need if d >= abs(delta)) for delta in deltas}
    edge = 0
    for boundary in range(1, lat_count):
        edge = max(edge, distance(boundary * rows - 1), distance(boundary * rows))
    halo = [d for d in range(1 - lon_count // 2, lon_count // 2 + 1) if abs(d) <= edge]
    groups = [(rows // 2, rows), (rows // 4, rows // 2), (0, rows // 4)]
    stages = []
    upper = rows
    for low, _ in groups:
        lower = max(low - 1, 0)
        stage = []
        for delta in sorted(deltas, key=lambda d: -abs(d)):
            if min(counts[delta], upper) > lower:
                stage.append(("block", delta, lower, min(counts[delta], upper)))
        stages.append(stage)
        upper = lower
    if lat_count > 1:
        stages[0] = [(side, d, 0, 1) for d in halo for side in ("down", "up")] + stages[0]
    return groups, stages, counts, halo


def block_kernel(
    lon_count,
    lat_count,
    plan,
    x_ref,
    rows_ref,
    lons_ref,
    weights_ref,
    gain_ref,
    mix_hbm,
    up_hbm,
    down_hbm,
    out_ref,
    window,
    filters,
    product,
    mix_ref,
    up_ref,
    down_ref,
    send_sem,
    recv_sem,
    load_sem,
):
    rows, cols, channels = x_ref.shape
    bases, entries = rows_ref.shape[:2]
    lon_total = lon_count * cols
    middle = lon_count // 2
    groups, stages, counts, halo = plan
    me, lat = lax.axis_index("lon"), lax.axis_index("lat")
    north = 2 * lat < lat_count
    has_low, has_high = lat > 0, lat < lat_count - 1

    loads = [
        pltpu.make_async_copy(mix_hbm, mix_ref, load_sem.at[0]),
        pltpu.make_async_copy(up_hbm, up_ref, load_sem.at[1]),
        pltpu.make_async_copy(down_hbm, down_ref, load_sem.at[2]),
    ]
    for load in loads:
        load.start()

    barrier = pltpu.get_barrier_semaphore()
    halo_deltas = halo if lat_count > 1 else []
    for delta in range(1, lon_count):
        pl.semaphore_signal(
            barrier, inc=1, device_id={"lon": lax.rem(me + delta, lon_count)}, device_id_type=MESH
        )
    for present, other in ((has_low, lat - 1), (has_high, lat + 1)):

        @pl.when(present)
        def _():
            for delta in halo_deltas:
                target = lax.rem(me + lon_count - delta, lon_count)
                pl.semaphore_signal(
                    barrier, inc=1, device_id={"lon": target, "lat": other}, device_id_type=MESH
                )

    sides = jnp.where(has_low, 1, 0) + jnp.where(has_high, 1, 0)
    pl.semaphore_wait(barrier, lon_count - 1 + sides * len(halo_deltas))

    def copy_of(index, item):
        kind, delta, first, last = item
        target = lax.rem(me + lon_count - delta, lon_count)
        slot = (delta + middle) % lon_count
        if kind == "block":
            start = jnp.where(north, first, rows - last)
            source = x_ref.at[pl.ds(start, last - first)]
            landing = window.at[pl.ds(start + 1, last - first), pl.ds(slot * cols, cols)]
            device = {"lon": target}
        elif kind == "down":
            source = x_ref.at[pl.ds(rows - 1, 1)]
            landing = window.at[pl.ds(0, 1), pl.ds(slot * cols, cols)]
            device = {"lon": target, "lat": jnp.minimum(lat + 1, lat_count - 1)}
        else:
            source = x_ref.at[pl.ds(0, 1)]
            landing = window.at[pl.ds(rows + 1, 1), pl.ds(slot * cols, cols)]
            device = {"lon": target, "lat": jnp.maximum(lat - 1, 0)}
        return pltpu.make_async_remote_copy(
            src_ref=source,
            dst_ref=landing,
            send_sem=send_sem.at[index],
            recv_sem=recv_sem.at[index],
            device_id=device,
            device_id_type=MESH,
        )

    copies = []
    for stage in stages:
        copies.append(list(enumerate(stage, sum(len(done) for done in copies))))

    def each(items, sending, action):
        for index, item in items:
            if item[0] == "block":
                action(copy_of(index, item))
            else:
                present = has_high if (item[0] == "down") == sending else has_low

                @pl.when(present)
                def _():
                    action(copy_of(index, item))

    for stage in copies:
        each(stage, True, lambda copy: copy.start())

    window[1 : rows + 1, middle * cols : (middle + 1) * cols, :] = x_ref[...]
    for delta, count in counts.items():
        slot = (delta + middle) % lon_count
        if count < rows:
            gap = (rows - count, cols, channels)
            window[pl.ds(jnp.where(north, count, 0) + 1, rows - count),
                   slot * cols : (slot + 1) * cols] = jnp.zeros(gap, jnp.bfloat16)
    for present, line in ((has_low, 0), (has_high, rows + 1)):
        for delta in range(1 - middle, middle + 1):
            slot = (delta + middle) % lon_count

            def clear():
                window[line, slot * cols : (slot + 1) * cols] = jnp.zeros(
                    (cols, channels), jnp.bfloat16
                )

            if delta in halo and lat_count > 1:
                pl.when(jnp.logical_not(present))(clear)
            else:
                clear()

    lanes = lax.broadcasted_iota(jnp.int32, (rows, lon_total), 1)
    wide = (rows, rows_ref.shape[2])
    own_rows = (
        lax.broadcasted_iota(jnp.int32, wide, 0) + lat * rows
        == lax.broadcasted_iota(jnp.int32, wide, 1)
    ).astype(jnp.float32)

    def own(ref, k):
        return lax.dot_general(
            own_rows,
            ref[k].astype(jnp.float32),
            (((1,), (1,)), ((), ())),
            precision=lax.Precision.HIGHEST,
            preferred_element_type=jnp.float32,
        )

    def build(k, carry):
        spot = own(lons_ref, k).astype(jnp.int32) + middle * cols
        spot = jnp.where(spot >= lon_total, spot - lon_total, spot)
        row_offset = own(rows_ref, k)
        weight = own(weights_ref, k)
        picked = [jnp.where(row_offset == r, weight, 0.0) for r in (-1.0, 0.0, 1.0)]
        sums = [jnp.zeros((rows, lon_total), jnp.float32) for _ in range(3)]
        for s in range(entries):
            hit = spot[:, s : s + 1] == lanes
            for r in range(3):
                sums[r] = sums[r] + jnp.where(hit, picked[r][:, s : s + 1], 0.0)
        for r in range(3):
            for i in range(rows):
                line = jnp.broadcast_to(sums[r][i : i + 1, :], (cols, lon_total))
                turned = pltpu.roll(line, 0, 1, stride=1, stride_axis=0)
                filters[i, pl.ds(pl.multiple_of(k * cols, cols), cols),
                        r * lon_total : (r + 1) * lon_total] = turned.astype(jnp.bfloat16)
        return carry

    lax.fori_loop(0, bases, build, 0)

    def group(low, high):
        start = jnp.where(north, low, rows - high)
        half = high - low
        lines = half * cols
        def filter_row(t, carry):
            i = start + t
            source = window[pl.ds(i, 3)].reshape(3 * lon_total, channels)
            filtered = jnp.dot(filters[i], source, preferred_element_type=jnp.float32)
            filtered = filtered.astype(jnp.bfloat16)
            at = pl.multiple_of(t * cols, cols)
            for k in range(bases):
                product[pl.ds(at, cols), k * channels : (k + 1) * channels] = filtered[
                    k * cols : (k + 1) * cols
                ]
            return carry

        lax.fori_loop(0, half, filter_row, 0)
        mixed = jnp.dot(product[:lines], mix_ref[...], preferred_element_type=jnp.float32)
        here = x_ref[pl.ds(start, half)].reshape(lines, channels)
        latent = here.astype(jnp.float32) + mixed
        mean = jnp.mean(latent, axis=1, keepdims=True)
        centred = latent - mean
        variance = jnp.mean(centred * centred, axis=1, keepdims=True)
        normed = (centred * lax.rsqrt(variance + norm_eps) * gain_ref[...][None, :]).astype(jnp.bfloat16)
        raised = jnp.dot(normed, up_ref[...], preferred_element_type=jnp.float32)
        hidden = 0.5 * raised * (1.0 + lax.erf(raised * math.sqrt(0.5)))
        lowered = jnp.dot(
            hidden.astype(jnp.bfloat16), down_ref[...], preferred_element_type=jnp.float32
        )
        result = (latent + lowered).astype(jnp.bfloat16)
        out_ref[pl.ds(start, half)] = result.reshape(half, cols, channels)

    for stage, (low, high) in zip(copies, groups):
        each(stage, False, lambda copy: copy.wait_recv())
        if stage is copies[0]:
            for load in loads:
                load.wait()
        group(low, high)
    for stage in copies:
        each(stage, True, lambda copy: copy.wait_send())


def on_device(
    lon_count,
    lat_count,
    fields,
    support_rows,
    support_lons,
    support_weights,
    mix_weight,
    norm_gain,
    up_weight,
    down_weight,
):
    channels, rows, cols = fields.shape
    bases, hidden = mix_weight.shape[0], up_weight.shape[1]
    lon_total = lon_count * cols
    plan = plan_copies(lon_count, lat_count, rows, cols)
    count = sum(len(stage) for stage in plan[1])
    in_vmem = pl.BlockSpec(memory_space=pltpu.VMEM)
    anywhere = pl.BlockSpec(memory_space=pl.ANY)
    result = pl.pallas_call(
        functools.partial(block_kernel, lon_count, lat_count, plan),
        out_shape=jax.ShapeDtypeStruct((rows, cols, channels), jnp.bfloat16),
        in_specs=[in_vmem] * 5 + [anywhere] * 3,
        out_specs=in_vmem,
        scratch_shapes=[
            pltpu.VMEM((rows + 2, lon_total, channels), jnp.bfloat16),
            pltpu.VMEM((rows, bases * cols, 3 * lon_total), jnp.bfloat16),
            pltpu.VMEM((rows // 2 * cols, bases * channels), jnp.bfloat16),
            pltpu.VMEM((bases * channels, channels), jnp.bfloat16),
            pltpu.VMEM((channels, hidden), jnp.bfloat16),
            pltpu.VMEM((hidden, channels), jnp.bfloat16),
            pltpu.SemaphoreType.DMA((count,)),
            pltpu.SemaphoreType.DMA((count,)),
            pltpu.SemaphoreType.DMA((3,)),
        ],
        compiler_params=pltpu.CompilerParams(
            collective_id=0, has_side_effects=True, vmem_limit_bytes=56 * 1024 * 1024
        ),
    )(
        jnp.transpose(fields, (1, 2, 0)),
        jnp.transpose(support_rows, (0, 2, 1)),
        jnp.transpose(support_lons, (0, 2, 1)),
        jnp.transpose(support_weights, (0, 2, 1)),
        norm_gain,
        mix_weight.reshape(bases * channels, channels),
        up_weight,
        down_weight,
    )
    return jnp.transpose(result, (2, 0, 1))


def solution(mesh):
    in_specs = (P("member", "lat", "lon"), P(), P(), P(), P(), P(), P(), P())
    out_specs = P("member", "lat", "lon")
    return jax.shard_map(
        functools.partial(on_device, mesh.shape["lon"], mesh.shape["lat"]),
        mesh=mesh,
        in_specs=in_specs,
        out_specs=out_specs,
        check_vma=False,
    )
```

```python
import functools
import math

import jax
import jax.numpy as jnp
from jax import lax
from jax.experimental import pallas as pl
from jax.experimental.pallas import tpu as pltpu
from jax.sharding import PartitionSpec as P

norm_eps = 1e-05
MESH = pl.DeviceIdType.MESH


def plan_copies(lon_count, lat_count, rows, cols):
    lon_total, row_total = lon_count * cols, lat_count * rows

    def distance(row):
        nearest = min(row + 1, row_total - row)
        reach = min(lon_total // 2, 4 * row_total // nearest)
        return min(-(-reach // cols), lon_count // 2)

    need = [distance(max(p - 1, 0)) for p in range(rows)]
    deltas = [d for d in range(1 - lon_count // 2, lon_count // 2 + 1) if d != 0]
    counts = {delta: sum(1 for d in need if d >= abs(delta)) for delta in deltas}
    edge = 0
    for boundary in range(1, lat_count):
        edge = max(edge, distance(boundary * rows - 1), distance(boundary * rows))
    halo = [d for d in range(1 - lon_count // 2, lon_count // 2 + 1) if abs(d) <= edge]
    groups = [(rows // 2, rows), (rows // 4, rows // 2), (0, rows // 4)]
    stages = []
    upper = rows
    for low, _ in groups:
        lower = max(low - 1, 0)
        stage = []
        for delta in sorted(deltas, key=lambda d: -abs(d)):
            if min(counts[delta], upper) > lower:
                stage.append(("block", delta, lower, min(counts[delta], upper)))
        stages.append(stage)
        upper = lower
    if lat_count > 1:
        stages[0] = [(side, d, 0, 1) for d in halo for side in ("down", "up")] + stages[0]
    return groups, stages, counts, halo


def block_kernel(
    lon_count,
    lat_count,
    plan,
    x_ref,
    rows_ref,
    lons_ref,
    weights_ref,
    gain_ref,
    mix_hbm,
    up_hbm,
    down_hbm,
    out_ref,
    window,
    filters,
    product,
    mix_ref,
    up_ref,
    down_ref,
    send_sem,
    recv_sem,
    relay_sem,
    load_sem,
):
    rows, cols, channels = x_ref.shape
    bases, entries = rows_ref.shape[:2]
    lon_total = lon_count * cols
    middle = lon_count // 2
    groups, stages, counts, halo = plan
    me, lat = lax.axis_index("lon"), lax.axis_index("lat")
    north = 2 * lat < lat_count
    has_low, has_high = lat > 0, lat < lat_count - 1

    loads = [
        pltpu.make_async_copy(mix_hbm, mix_ref, load_sem.at[0]),
        pltpu.make_async_copy(up_hbm, up_ref, load_sem.at[1]),
        pltpu.make_async_copy(down_hbm, down_ref, load_sem.at[2]),
    ]
    for load in loads:
        load.start()

    barrier = pltpu.get_barrier_semaphore()
    halo_deltas = halo if lat_count > 1 else []
    for delta in range(1, lon_count):
        pl.semaphore_signal(
            barrier, inc=1, device_id={"lon": lax.rem(me + delta, lon_count)}, device_id_type=MESH
        )
    for present, other in ((has_low, lat - 1), (has_high, lat + 1)):

        @pl.when(present)
        def _():
            for delta in halo_deltas:
                target = lax.rem(me + lon_count - delta, lon_count)
                pl.semaphore_signal(
                    barrier, inc=1, device_id={"lon": target, "lat": other}, device_id_type=MESH
                )

    sides = jnp.where(has_low, 1, 0) + jnp.where(has_high, 1, 0)
    pl.semaphore_wait(barrier, lon_count - 1 + sides * len(halo_deltas))

    def copy_of(index, item):
        kind, delta, first, last = item
        target = lax.rem(me + lon_count - delta, lon_count)
        slot = (delta + middle) % lon_count
        if kind == "block":
            start = jnp.where(north, first, rows - last)
            source = x_ref.at[pl.ds(start, last - first)]
            landing = window.at[pl.ds(start + 1, last - first), pl.ds(slot * cols, cols)]
            device = {"lon": target}
        elif kind == "down":
            source = x_ref.at[pl.ds(rows - 1, 1)]
            landing = window.at[pl.ds(0, 1), pl.ds(slot * cols, cols)]
            device = {"lon": target, "lat": jnp.minimum(lat + 1, lat_count - 1)}
        else:
            source = x_ref.at[pl.ds(0, 1)]
            landing = window.at[pl.ds(rows + 1, 1), pl.ds(slot * cols, cols)]
            device = {"lon": target, "lat": jnp.maximum(lat - 1, 0)}
        return pltpu.make_async_remote_copy(
            src_ref=source,
            dst_ref=landing,
            send_sem=send_sem.at[index],
            recv_sem=recv_sem.at[index],
            device_id=device,
            device_id_type=MESH,
        )

    copies = []
    for stage in stages:
        copies.append(list(enumerate(stage, sum(len(done) for done in copies))))

    flat = [pair for stage in copies for pair in stage]
    odd = lax.rem(me, 2) == 1
    even = lax.rem(me, 2) == 0

    def direct_sender(item):
        delta = item[1]
        if delta % 2 == 0:
            return (even, odd)
        return (odd,) if delta == 1 else (even,) if delta == -1 else ()

    def direct_receiver(item):
        delta = item[1]
        return (even,) if delta == 1 else (odd,) if delta == -1 else ()

    def side_present(item, sending):
        if item[0] == "block":
            return None
        return has_high if (item[0] == "down") == sending else has_low

    def guarded(conditions, action):
        conditions = [c for c in conditions if c is not None]
        if not conditions:
            action()
        else:
            pl.when(functools.reduce(jnp.logical_and, conditions))(action)

    def window_part(item, slot_start):
        kind, _, first, last = item
        if kind == "block":
            start = jnp.where(north, first, rows - last) + 1
        else:
            start = 0 if kind == "down" else rows + 1
        return window.at[pl.ds(start, last - first), pl.ds(slot_start, cols)]

    def receiver_side(item):
        return has_low if item[0] == "down" else has_high if item[0] == "up" else None

    def relay_of(index, item, target, held):
        source = pl.multiple_of((middle + held) * cols, cols)
        landing = ((item[1] + middle) % lon_count) * cols
        return pltpu.make_async_remote_copy(
            src_ref=window_part(item, source),
            dst_ref=window_part(item, landing),
            send_sem=relay_sem.at[index],
            recv_sem=recv_sem.at[index],
            device_id={"lon": target},
            device_id_type=MESH,
        )

    def relay_action(index, item, action):
        kind, delta, first, last = item
        if delta % 2 == 0:
            return
        present = receiver_side(item)
        if abs(delta) == 1 and kind == "block" and last <= counts[2] and last < rows:
            parity = even if delta == 1 else odd
            target = lax.rem(me + lon_count + delta, lon_count)
            guarded([parity], lambda: action(relay_of(index, item, target, 2 * delta)))
            return
        for parity, own_delta in ((even, 1), (odd, -1)):
            if delta == own_delta:
                continue
            target = lax.rem(me + 2 * lon_count - delta + own_delta, lon_count)
            guarded(
                [parity, present],
                lambda: action(relay_of(index, item, target, own_delta)),
            )

    def send_direct(action):
        for index, item in flat:
            parities = direct_sender(item)
            if len(parities) == 2:
                guarded([side_present(item, True)], lambda: action(copy_of(index, item)))
            else:
                for parity in parities:
                    guarded(
                        [parity, side_present(item, True)],
                        lambda: action(copy_of(index, item)),
                    )

    def await_direct(stage):
        for index, item in stage:
            if item[1] in (2, -2) and item[0] == "block":
                copy_of(index, item).wait_recv()
            for parity in direct_receiver(item):
                guarded(
                    [parity, side_present(item, False)],
                    lambda: copy_of(index, item).wait_recv(),
                )

    def await_rest(stage):
        for index, item in stage:
            side = side_present(item, False)
            if item[1] in (2, -2) and item[0] == "block":
                continue
            if item[1] in (1, -1):
                other = odd if item[1] == 1 else even
                guarded([other, side], lambda: copy_of(index, item).wait_recv())
            else:
                guarded([side], lambda: copy_of(index, item).wait_recv())

    send_direct(lambda copy: copy.start())

    window[1 : rows + 1, middle * cols : (middle + 1) * cols, :] = x_ref[...]
    for delta, count in counts.items():
        slot = (delta + middle) % lon_count
        if count < rows:
            gap = (rows - count, cols, channels)
            window[pl.ds(jnp.where(north, count, 0) + 1, rows - count),
                   slot * cols : (slot + 1) * cols] = jnp.zeros(gap, jnp.bfloat16)
    for present, line in ((has_low, 0), (has_high, rows + 1)):
        for delta in range(1 - middle, middle + 1):
            slot = (delta + middle) % lon_count

            def clear():
                window[line, slot * cols : (slot + 1) * cols] = jnp.zeros(
                    (cols, channels), jnp.bfloat16
                )

            if delta in halo and lat_count > 1:
                pl.when(jnp.logical_not(present))(clear)
            else:
                clear()

    lanes = lax.broadcasted_iota(jnp.int32, (rows, lon_total), 1)
    wide = (rows, rows_ref.shape[2])
    own_rows = (
        lax.broadcasted_iota(jnp.int32, wide, 0) + lat * rows
        == lax.broadcasted_iota(jnp.int32, wide, 1)
    ).astype(jnp.float32)

    def own(ref, k):
        return lax.dot_general(
            own_rows,
            ref[k].astype(jnp.float32),
            (((1,), (1,)), ((), ())),
            precision=lax.Precision.HIGHEST,
            preferred_element_type=jnp.float32,
        )

    def build(k, carry):
        spot = own(lons_ref, k).astype(jnp.int32) + middle * cols
        spot = jnp.where(spot >= lon_total, spot - lon_total, spot)
        row_offset = own(rows_ref, k)
        weight = own(weights_ref, k)
        picked = [jnp.where(row_offset == r, weight, 0.0) for r in (-1.0, 0.0, 1.0)]
        sums = [jnp.zeros((rows, lon_total), jnp.float32) for _ in range(3)]
        for s in range(entries):
            hit = spot[:, s : s + 1] == lanes
            for r in range(3):
                sums[r] = sums[r] + jnp.where(hit, picked[r][:, s : s + 1], 0.0)
        for r in range(3):
            for i in range(rows):
                line = jnp.broadcast_to(sums[r][i : i + 1, :], (cols, lon_total))
                turned = pltpu.roll(line, 0, 1, stride=1, stride_axis=0)
                filters[i, pl.ds(pl.multiple_of(k * cols, cols), cols),
                        r * lon_total : (r + 1) * lon_total] = turned.astype(jnp.bfloat16)
        return carry

    lax.fori_loop(0, bases, build, 0)

    for stage in copies:
        await_direct(stage)
        for index, item in stage:
            relay_action(index, item, lambda copy: copy.start())

    def group(low, high):
        start = jnp.where(north, low, rows - high)
        half = high - low
        lines = half * cols
        def filter_row(t, carry):
            i = start + t
            source = window[pl.ds(i, 3)].reshape(3 * lon_total, channels)
            filtered = jnp.dot(filters[i], source, preferred_element_type=jnp.float32)
            filtered = filtered.astype(jnp.bfloat16)
            at = pl.multiple_of(t * cols, cols)
            for k in range(bases):
                product[pl.ds(at, cols), k * channels : (k + 1) * channels] = filtered[
                    k * cols : (k + 1) * cols
                ]
            return carry

        lax.fori_loop(0, half, filter_row, 0)
        mixed = jnp.dot(product[:lines], mix_ref[...], preferred_element_type=jnp.float32)
        here = x_ref[pl.ds(start, half)].reshape(lines, channels)
        latent = here.astype(jnp.float32) + mixed
        mean = jnp.mean(latent, axis=1, keepdims=True)
        centred = latent - mean
        variance = jnp.mean(centred * centred, axis=1, keepdims=True)
        normed = (centred * lax.rsqrt(variance + norm_eps) * gain_ref[...][None, :]).astype(jnp.bfloat16)
        raised = jnp.dot(normed, up_ref[...], preferred_element_type=jnp.float32)
        hidden = 0.5 * raised * (1.0 + lax.erf(raised * math.sqrt(0.5)))
        lowered = jnp.dot(
            hidden.astype(jnp.bfloat16), down_ref[...], preferred_element_type=jnp.float32
        )
        result = (latent + lowered).astype(jnp.bfloat16)
        out_ref[pl.ds(start, half)] = result.reshape(half, cols, channels)

    for stage, (low, high) in zip(copies, groups):
        await_rest(stage)
        if stage is copies[0]:
            for load in loads:
                load.wait()
        group(low, high)
    send_direct(lambda copy: copy.wait_send())
    for index, item in flat:
        relay_action(index, item, lambda copy: copy.wait_send())


def on_device(
    lon_count,
    lat_count,
    fields,
    support_rows,
    support_lons,
    support_weights,
    mix_weight,
    norm_gain,
    up_weight,
    down_weight,
):
    channels, rows, cols = fields.shape
    bases, hidden = mix_weight.shape[0], up_weight.shape[1]
    lon_total = lon_count * cols
    plan = plan_copies(lon_count, lat_count, rows, cols)
    count = sum(len(stage) for stage in plan[1])
    in_vmem = pl.BlockSpec(memory_space=pltpu.VMEM)
    anywhere = pl.BlockSpec(memory_space=pl.ANY)
    result = pl.pallas_call(
        functools.partial(block_kernel, lon_count, lat_count, plan),
        out_shape=jax.ShapeDtypeStruct((rows, cols, channels), jnp.bfloat16),
        in_specs=[in_vmem] * 5 + [anywhere] * 3,
        out_specs=in_vmem,
        scratch_shapes=[
            pltpu.VMEM((rows + 2, lon_total, channels), jnp.bfloat16),
            pltpu.VMEM((rows, bases * cols, 3 * lon_total), jnp.bfloat16),
            pltpu.VMEM((rows // 2 * cols, bases * channels), jnp.bfloat16),
            pltpu.VMEM((bases * channels, channels), jnp.bfloat16),
            pltpu.VMEM((channels, hidden), jnp.bfloat16),
            pltpu.VMEM((hidden, channels), jnp.bfloat16),
            pltpu.SemaphoreType.DMA((count,)),
            pltpu.SemaphoreType.DMA((count,)),
            pltpu.SemaphoreType.DMA((count,)),
            pltpu.SemaphoreType.DMA((3,)),
        ],
        compiler_params=pltpu.CompilerParams(
            collective_id=0, has_side_effects=True, vmem_limit_bytes=56 * 1024 * 1024
        ),
    )(
        jnp.transpose(fields, (1, 2, 0)),
        jnp.transpose(support_rows, (0, 2, 1)),
        jnp.transpose(support_lons, (0, 2, 1)),
        jnp.transpose(support_weights, (0, 2, 1)),
        norm_gain,
        mix_weight.reshape(bases * channels, channels),
        up_weight,
        down_weight,
    )
    return jnp.transpose(result, (2, 0, 1))


def solution(mesh):
    in_specs = (P("member", "lat", "lon"), P(), P(), P(), P(), P(), P(), P())
    out_specs = P("member", "lat", "lon")
    return jax.shard_map(
        functools.partial(on_device, mesh.shape["lon"], mesh.shape["lat"]),
        mesh=mesh,
        in_specs=in_specs,
        out_specs=out_specs,
        check_vma=False,
    )
```

```python
import functools
import math

import jax
import jax.numpy as jnp
from jax import lax
from jax.experimental import pallas as pl
from jax.experimental.pallas import tpu as pltpu
from jax.sharding import PartitionSpec as P

norm_eps = 1e-05
MESH = pl.DeviceIdType.MESH


def plan_copies(lon_count, lat_count, rows, cols):
    lon_total, row_total = lon_count * cols, lat_count * rows

    def reach(row):
        nearest = min(row + 1, row_total - row)
        return min(lon_total // 2, 4 * row_total // nearest)

    def distance(row):
        return min(-(-reach(row) // cols), lon_count // 2)

    def in_half(span, delta):
        if delta == 0 or abs(delta) == lon_count // 2:
            return False
        return span - cols * (abs(delta) - 1) <= cols // 2

    need = [distance(max(p - 1, 0)) for p in range(rows)]
    deltas = [d for d in range(1 - lon_count // 2, lon_count // 2 + 1) if d != 0]
    counts = {delta: sum(1 for d in need if d >= abs(delta)) for delta in deltas}
    spans = [reach(max(p - 1, 0)) for p in range(rows)]
    fulls = {d: sum(1 for p in range(counts[d]) if not in_half(spans[p], d)) for d in deltas}
    edge, edge_span = 0, 0
    for boundary in range(1, lat_count):
        edge = max(edge, distance(boundary * rows - 1), distance(boundary * rows))
        edge_span = max(edge_span, reach(boundary * rows - 1), reach(boundary * rows))
    halo = [d for d in range(1 - lon_count // 2, lon_count // 2 + 1) if abs(d) <= edge]
    groups = [(rows // 2, rows), (rows // 4, rows // 2), (0, rows // 4)]
    stages = []
    upper = rows
    for low, _ in groups:
        lower = max(low - 1, 0)
        stage = []
        for delta in sorted(deltas, key=lambda d: -abs(d)):
            full, top = min(fulls[delta], upper), min(counts[delta], upper)
            if full > lower:
                stage.append(("block", delta, lower, full, False))
            if top > max(full, lower):
                stage.append(("block", delta, max(full, lower), top, True))
        stages.append(stage)
        upper = lower
    if lat_count > 1:
        stages[0] = [
            (side, d, 0, 1, in_half(edge_span, d)) for d in halo for side in ("down", "up")
        ] + stages[0]
    halves = [d for d in halo if in_half(edge_span, d)]
    return groups, stages, counts, fulls, halo, halves


def block_kernel(
    lon_count,
    lat_count,
    plan,
    x_ref,
    rows_ref,
    lons_ref,
    weights_ref,
    gain_ref,
    mix_hbm,
    up_hbm,
    down_hbm,
    out_ref,
    window,
    filters,
    product,
    mix_ref,
    up_ref,
    down_ref,
    send_sem,
    recv_sem,
    load_sem,
):
    rows, cols, channels = x_ref.shape
    bases, entries = rows_ref.shape[:2]
    lon_total = lon_count * cols
    middle = lon_count // 2
    groups, stages, counts, fulls, halo, halves = plan
    me, lat = lax.axis_index("lon"), lax.axis_index("lat")
    north = 2 * lat < lat_count
    has_low, has_high = lat > 0, lat < lat_count - 1

    loads = [
        pltpu.make_async_copy(mix_hbm, mix_ref, load_sem.at[0]),
        pltpu.make_async_copy(up_hbm, up_ref, load_sem.at[1]),
        pltpu.make_async_copy(down_hbm, down_ref, load_sem.at[2]),
    ]
    for load in loads:
        load.start()

    barrier = pltpu.get_barrier_semaphore()
    halo_deltas = halo if lat_count > 1 else []
    for delta in range(1, lon_count):
        pl.semaphore_signal(
            barrier, inc=1, device_id={"lon": lax.rem(me + delta, lon_count)}, device_id_type=MESH
        )
    for present, other in ((has_low, lat - 1), (has_high, lat + 1)):

        @pl.when(present)
        def _():
            for delta in halo_deltas:
                target = lax.rem(me + lon_count - delta, lon_count)
                pl.semaphore_signal(
                    barrier, inc=1, device_id={"lon": target, "lat": other}, device_id_type=MESH
                )

    sides = jnp.where(has_low, 1, 0) + jnp.where(has_high, 1, 0)
    pl.semaphore_wait(barrier, lon_count - 1 + sides * len(halo_deltas))

    def copy_of(index, item):
        kind, delta, first, last, halved = item
        width = cols // 2 if halved else cols
        offset = cols // 2 if halved and delta < 0 else 0
        target = lax.rem(me + lon_count - delta, lon_count)
        slot = (delta + middle) % lon_count
        here, there = pl.ds(offset, width), pl.ds(slot * cols + offset, width)
        if kind == "block":
            start = jnp.where(north, first, rows - last)
            source = x_ref.at[pl.ds(start, last - first), here]
            landing = window.at[pl.ds(start + 1, last - first), there]
            device = {"lon": target}
        elif kind == "down":
            source = x_ref.at[pl.ds(rows - 1, 1), here]
            landing = window.at[pl.ds(0, 1), there]
            device = {"lon": target, "lat": jnp.minimum(lat + 1, lat_count - 1)}
        else:
            source = x_ref.at[pl.ds(0, 1), here]
            landing = window.at[pl.ds(rows + 1, 1), there]
            device = {"lon": target, "lat": jnp.maximum(lat - 1, 0)}
        return pltpu.make_async_remote_copy(
            src_ref=source,
            dst_ref=landing,
            send_sem=send_sem.at[index],
            recv_sem=recv_sem.at[index],
            device_id=device,
            device_id_type=MESH,
        )

    copies = []
    for stage in stages:
        copies.append(list(enumerate(stage, sum(len(done) for done in copies))))

    def each(items, sending, action):
        for index, item in items:
            if item[0] == "block":
                action(copy_of(index, item))
            else:
                present = has_high if (item[0] == "down") == sending else has_low

                @pl.when(present)
                def _():
                    action(copy_of(index, item))

    for stage in copies:
        each(stage, True, lambda copy: copy.start())

    window[1 : rows + 1, middle * cols : (middle + 1) * cols, :] = x_ref[...]
    for delta, count in counts.items():
        slot = (delta + middle) % lon_count
        if count < rows:
            gap = (rows - count, cols, channels)
            window[pl.ds(jnp.where(north, count, 0) + 1, rows - count),
                   slot * cols : (slot + 1) * cols] = jnp.zeros(gap, jnp.bfloat16)
        partial = count - fulls[delta]
        if partial > 0:
            far = slot * cols + (0 if delta < 0 else cols // 2)
            window[pl.ds(jnp.where(north, fulls[delta], rows - count) + 1, partial),
                   far : far + cols // 2] = jnp.zeros(
                (partial, cols // 2, channels), jnp.bfloat16
            )
    for delta in halves:
        far = (delta + middle) % lon_count * cols + (0 if delta < 0 else cols // 2)
        for line in (0, rows + 1):
            window[line, far : far + cols // 2] = jnp.zeros((cols // 2, channels), jnp.bfloat16)
    for present, line in ((has_low, 0), (has_high, rows + 1)):
        for delta in range(1 - middle, middle + 1):
            slot = (delta + middle) % lon_count

            def clear():
                window[line, slot * cols : (slot + 1) * cols] = jnp.zeros(
                    (cols, channels), jnp.bfloat16
                )

            if delta in halo and lat_count > 1:
                pl.when(jnp.logical_not(present))(clear)
            else:
                clear()

    lanes = lax.broadcasted_iota(jnp.int32, (rows, lon_total), 1)
    wide = (rows, rows_ref.shape[2])
    own_rows = (
        lax.broadcasted_iota(jnp.int32, wide, 0) + lat * rows
        == lax.broadcasted_iota(jnp.int32, wide, 1)
    ).astype(jnp.float32)

    def own(ref, k):
        return lax.dot_general(
            own_rows,
            ref[k].astype(jnp.float32),
            (((1,), (1,)), ((), ())),
            precision=lax.Precision.HIGHEST,
            preferred_element_type=jnp.float32,
        )

    def build(k, carry):
        spot = own(lons_ref, k).astype(jnp.int32) + middle * cols
        spot = jnp.where(spot >= lon_total, spot - lon_total, spot)
        row_offset = own(rows_ref, k)
        weight = own(weights_ref, k)
        picked = [jnp.where(row_offset == r, weight, 0.0) for r in (-1.0, 0.0, 1.0)]
        sums = [jnp.zeros((rows, lon_total), jnp.float32) for _ in range(3)]
        for s in range(entries):
            hit = spot[:, s : s + 1] == lanes
            for r in range(3):
                sums[r] = sums[r] + jnp.where(hit, picked[r][:, s : s + 1], 0.0)
        for r in range(3):
            for i in range(rows):
                line = jnp.broadcast_to(sums[r][i : i + 1, :], (cols, lon_total))
                turned = pltpu.roll(line, 0, 1, stride=1, stride_axis=0)
                filters[i, pl.ds(pl.multiple_of(k * cols, cols), cols),
                        r * lon_total : (r + 1) * lon_total] = turned.astype(jnp.bfloat16)
        return carry

    lax.fori_loop(0, bases, build, 0)

    def group(low, high):
        start = jnp.where(north, low, rows - high)
        half = high - low
        lines = half * cols
        def filter_row(t, carry):
            i = start + t
            source = window[pl.ds(i, 3)].reshape(3 * lon_total, channels)
            filtered = jnp.dot(filters[i], source, preferred_element_type=jnp.float32)
            filtered = filtered.astype(jnp.bfloat16)
            at = pl.multiple_of(t * cols, cols)
            for k in range(bases):
                product[pl.ds(at, cols), k * channels : (k + 1) * channels] = filtered[
                    k * cols : (k + 1) * cols
                ]
            return carry

        lax.fori_loop(0, half, filter_row, 0)
        mixed = jnp.dot(product[:lines], mix_ref[...], preferred_element_type=jnp.float32)
        here = x_ref[pl.ds(start, half)].reshape(lines, channels)
        latent = here.astype(jnp.float32) + mixed
        mean = jnp.mean(latent, axis=1, keepdims=True)
        centred = latent - mean
        variance = jnp.mean(centred * centred, axis=1, keepdims=True)
        normed = (centred * lax.rsqrt(variance + norm_eps) * gain_ref[...][None, :]).astype(jnp.bfloat16)
        raised = jnp.dot(normed, up_ref[...], preferred_element_type=jnp.float32)
        hidden = 0.5 * raised * (1.0 + lax.erf(raised * math.sqrt(0.5)))
        lowered = jnp.dot(
            hidden.astype(jnp.bfloat16), down_ref[...], preferred_element_type=jnp.float32
        )
        result = (latent + lowered).astype(jnp.bfloat16)
        out_ref[pl.ds(start, half)] = result.reshape(half, cols, channels)

    for stage, (low, high) in zip(copies, groups):
        each(stage, False, lambda copy: copy.wait_recv())
        if stage is copies[0]:
            for load in loads:
                load.wait()
        group(low, high)
    for stage in copies:
        each(stage, True, lambda copy: copy.wait_send())


def on_device(
    lon_count,
    lat_count,
    fields,
    support_rows,
    support_lons,
    support_weights,
    mix_weight,
    norm_gain,
    up_weight,
    down_weight,
):
    channels, rows, cols = fields.shape
    bases, hidden = mix_weight.shape[0], up_weight.shape[1]
    lon_total = lon_count * cols
    plan = plan_copies(lon_count, lat_count, rows, cols)
    count = sum(len(stage) for stage in plan[1])
    in_vmem = pl.BlockSpec(memory_space=pltpu.VMEM)
    anywhere = pl.BlockSpec(memory_space=pl.ANY)
    result = pl.pallas_call(
        functools.partial(block_kernel, lon_count, lat_count, plan),
        out_shape=jax.ShapeDtypeStruct((rows, cols, channels), jnp.bfloat16),
        in_specs=[in_vmem] * 5 + [anywhere] * 3,
        out_specs=in_vmem,
        scratch_shapes=[
            pltpu.VMEM((rows + 2, lon_total, channels), jnp.bfloat16),
            pltpu.VMEM((rows, bases * cols, 3 * lon_total), jnp.bfloat16),
            pltpu.VMEM((rows // 2 * cols, bases * channels), jnp.bfloat16),
            pltpu.VMEM((bases * channels, channels), jnp.bfloat16),
            pltpu.VMEM((channels, hidden), jnp.bfloat16),
            pltpu.VMEM((hidden, channels), jnp.bfloat16),
            pltpu.SemaphoreType.DMA((count,)),
            pltpu.SemaphoreType.DMA((count,)),
            pltpu.SemaphoreType.DMA((3,)),
        ],
        compiler_params=pltpu.CompilerParams(
            collective_id=0, has_side_effects=True, vmem_limit_bytes=56 * 1024 * 1024
        ),
    )(
        jnp.transpose(fields, (1, 2, 0)),
        jnp.transpose(support_rows, (0, 2, 1)),
        jnp.transpose(support_lons, (0, 2, 1)),
        jnp.transpose(support_weights, (0, 2, 1)),
        norm_gain,
        mix_weight.reshape(bases * channels, channels),
        up_weight,
        down_weight,
    )
    return jnp.transpose(result, (2, 0, 1))


def solution(mesh):
    in_specs = (P("member", "lat", "lon"), P(), P(), P(), P(), P(), P(), P())
    out_specs = P("member", "lat", "lon")
    return jax.shard_map(
        functools.partial(on_device, mesh.shape["lon"], mesh.shape["lat"]),
        mesh=mesh,
        in_specs=in_specs,
        out_specs=out_specs,
        check_vma=False,
    )
```

```python
import functools
import math

import jax
import jax.numpy as jnp
from jax import lax
from jax.experimental import pallas as pl
from jax.experimental.pallas import tpu as pltpu
from jax.sharding import PartitionSpec as P

norm_eps = 1e-05
MESH = pl.DeviceIdType.MESH


def plan_copies(lon_count, lat_count, rows, cols):
    lon_total, row_total = lon_count * cols, lat_count * rows

    def reach(row):
        nearest = min(row + 1, row_total - row)
        return min(lon_total // 2, 4 * row_total // nearest)

    def distance(row):
        return min(-(-reach(row) // cols), lon_count // 2)

    def in_half(span, delta):
        if delta == 0 or abs(delta) == lon_count // 2:
            return False
        return span - cols * (abs(delta) - 1) <= cols // 2

    need = [distance(max(p - 1, 0)) for p in range(rows)]
    deltas = [d for d in range(1 - lon_count // 2, lon_count // 2 + 1) if d != 0]
    counts = {delta: sum(1 for d in need if d >= abs(delta)) for delta in deltas}
    spans = [reach(max(p - 1, 0)) for p in range(rows)]
    fulls = {d: sum(1 for p in range(counts[d]) if not in_half(spans[p], d)) for d in deltas}
    edge, edge_span = 0, 0
    for boundary in range(1, lat_count):
        edge = max(edge, distance(boundary * rows - 1), distance(boundary * rows))
        edge_span = max(edge_span, reach(boundary * rows - 1), reach(boundary * rows))
    halo = [d for d in range(1 - lon_count // 2, lon_count // 2 + 1) if abs(d) <= edge]
    groups = [(rows // 2, rows), (rows // 4, rows // 2), (0, rows // 4)]
    stages = []
    upper = rows
    for low, _ in groups:
        lower = max(low - 1, 0)
        stage = []
        for delta in sorted(deltas, key=lambda d: -abs(d)):
            full, top = min(fulls[delta], upper), min(counts[delta], upper)
            if full > lower:
                stage.append(("block", delta, lower, full, False))
            if top > max(full, lower):
                stage.append(("block", delta, max(full, lower), top, True))
        stages.append(stage)
        upper = lower
    if lat_count > 1:
        stages[0] = [
            (side, d, 0, 1, in_half(edge_span, d)) for d in halo for side in ("down", "up")
        ] + stages[0]
    halves = [d for d in halo if in_half(edge_span, d)]
    return groups, stages, counts, fulls, halo, halves


def block_kernel(
    lon_count,
    lat_count,
    plan,
    x_hbm,
    rows_ref,
    lons_ref,
    weights_ref,
    gain_ref,
    mix_hbm,
    up_hbm,
    down_hbm,
    out_hbm,
    x_ref,
    out_ref,
    window,
    filters,
    product,
    mix_ref,
    up_ref,
    down_ref,
    send_sem,
    recv_sem,
    load_sem,
    out_sem,
):
    rows, cols, channels = x_ref.shape
    bases, entries = rows_ref.shape[:2]
    lon_total = lon_count * cols
    middle = lon_count // 2
    groups, stages, counts, fulls, halo, halves = plan
    me, lat = lax.axis_index("lon"), lax.axis_index("lat")
    north = 2 * lat < lat_count
    has_low, has_high = lat > 0, lat < lat_count - 1

    loads = [
        pltpu.make_async_copy(mix_hbm, mix_ref, load_sem.at[0]),
        pltpu.make_async_copy(up_hbm, up_ref, load_sem.at[1]),
        pltpu.make_async_copy(down_hbm, down_ref, load_sem.at[2]),
    ]
    fetch = pltpu.make_async_copy(x_hbm, x_ref, load_sem.at[3])
    fetch.start()

    barrier = pltpu.get_barrier_semaphore()
    halo_deltas = halo if lat_count > 1 else []
    for delta in range(1, lon_count):
        pl.semaphore_signal(
            barrier, inc=1, device_id={"lon": lax.rem(me + delta, lon_count)}, device_id_type=MESH
        )
    for present, other in ((has_low, lat - 1), (has_high, lat + 1)):

        @pl.when(present)
        def _():
            for delta in halo_deltas:
                target = lax.rem(me + lon_count - delta, lon_count)
                pl.semaphore_signal(
                    barrier, inc=1, device_id={"lon": target, "lat": other}, device_id_type=MESH
                )

    sides = jnp.where(has_low, 1, 0) + jnp.where(has_high, 1, 0)
    pl.semaphore_wait(barrier, lon_count - 1 + sides * len(halo_deltas))
    fetch.wait()

    def copy_of(index, item):
        kind, delta, first, last, halved = item
        width = cols // 2 if halved else cols
        offset = cols // 2 if halved and delta < 0 else 0
        target = lax.rem(me + lon_count - delta, lon_count)
        slot = (delta + middle) % lon_count
        here, there = pl.ds(offset, width), pl.ds(slot * cols + offset, width)
        if kind == "block":
            start = jnp.where(north, first, rows - last)
            source = x_ref.at[pl.ds(start, last - first), here]
            landing = window.at[pl.ds(start + 1, last - first), there]
            device = {"lon": target}
        elif kind == "down":
            source = x_ref.at[pl.ds(rows - 1, 1), here]
            landing = window.at[pl.ds(0, 1), there]
            device = {"lon": target, "lat": jnp.minimum(lat + 1, lat_count - 1)}
        else:
            source = x_ref.at[pl.ds(0, 1), here]
            landing = window.at[pl.ds(rows + 1, 1), there]
            device = {"lon": target, "lat": jnp.maximum(lat - 1, 0)}
        return pltpu.make_async_remote_copy(
            src_ref=source,
            dst_ref=landing,
            send_sem=send_sem.at[index],
            recv_sem=recv_sem.at[index],
            device_id=device,
            device_id_type=MESH,
        )

    copies = []
    for stage in stages:
        copies.append(list(enumerate(stage, sum(len(done) for done in copies))))

    def each(items, sending, action):
        for index, item in items:
            if item[0] == "block":
                action(copy_of(index, item))
            else:
                present = has_high if (item[0] == "down") == sending else has_low

                @pl.when(present)
                def _():
                    action(copy_of(index, item))

    for stage in copies:
        each(stage, True, lambda copy: copy.start())
    for load in loads:
        load.start()

    window[1 : rows + 1, middle * cols : (middle + 1) * cols, :] = x_ref[...]
    for delta, count in counts.items():
        slot = (delta + middle) % lon_count
        if count < rows:
            gap = (rows - count, cols, channels)
            window[pl.ds(jnp.where(north, count, 0) + 1, rows - count),
                   slot * cols : (slot + 1) * cols] = jnp.zeros(gap, jnp.bfloat16)
        partial = count - fulls[delta]
        if partial > 0:
            far = slot * cols + (0 if delta < 0 else cols // 2)
            window[pl.ds(jnp.where(north, fulls[delta], rows - count) + 1, partial),
                   far : far + cols // 2] = jnp.zeros(
                (partial, cols // 2, channels), jnp.bfloat16
            )
    for delta in halves:
        far = (delta + middle) % lon_count * cols + (0 if delta < 0 else cols // 2)
        for line in (0, rows + 1):
            window[line, far : far + cols // 2] = jnp.zeros((cols // 2, channels), jnp.bfloat16)
    for present, line in ((has_low, 0), (has_high, rows + 1)):
        for delta in range(1 - middle, middle + 1):
            slot = (delta + middle) % lon_count

            def clear():
                window[line, slot * cols : (slot + 1) * cols] = jnp.zeros(
                    (cols, channels), jnp.bfloat16
                )

            if delta in halo and lat_count > 1:
                pl.when(jnp.logical_not(present))(clear)
            else:
                clear()

    lanes = lax.broadcasted_iota(jnp.int32, (rows, lon_total), 1)
    wide = (rows, rows_ref.shape[2])
    own_rows = (
        lax.broadcasted_iota(jnp.int32, wide, 0) + lat * rows
        == lax.broadcasted_iota(jnp.int32, wide, 1)
    ).astype(jnp.float32)

    def own(ref, k):
        return lax.dot_general(
            own_rows,
            ref[k].astype(jnp.float32),
            (((1,), (1,)), ((), ())),
            precision=lax.Precision.HIGHEST,
            preferred_element_type=jnp.float32,
        )

    def build(k, carry):
        spot = own(lons_ref, k).astype(jnp.int32) + middle * cols
        spot = jnp.where(spot >= lon_total, spot - lon_total, spot)
        row_offset = own(rows_ref, k)
        weight = own(weights_ref, k)
        picked = [jnp.where(row_offset == r, weight, 0.0) for r in (-1.0, 0.0, 1.0)]
        sums = [jnp.zeros((rows, lon_total), jnp.float32) for _ in range(3)]
        for s in range(entries):
            hit = spot[:, s : s + 1] == lanes
            for r in range(3):
                sums[r] = sums[r] + jnp.where(hit, picked[r][:, s : s + 1], 0.0)
        for r in range(3):
            for i in range(rows):
                line = jnp.broadcast_to(sums[r][i : i + 1, :], (cols, lon_total))
                turned = pltpu.roll(line, 0, 1, stride=1, stride_axis=0)
                filters[i, pl.ds(pl.multiple_of(k * cols, cols), cols),
                        r * lon_total : (r + 1) * lon_total] = turned.astype(jnp.bfloat16)
        return carry

    lax.fori_loop(0, bases, build, 0)

    def group(low, high):
        start = jnp.where(north, low, rows - high)
        half = high - low
        lines = half * cols
        def filter_row(t, carry):
            i = start + t
            source = window[pl.ds(i, 3)].reshape(3 * lon_total, channels)
            filtered = jnp.dot(filters[i], source, preferred_element_type=jnp.float32)
            filtered = filtered.astype(jnp.bfloat16)
            at = pl.multiple_of(t * cols, cols)
            for k in range(bases):
                product[pl.ds(at, cols), k * channels : (k + 1) * channels] = filtered[
                    k * cols : (k + 1) * cols
                ]
            return carry

        lax.fori_loop(0, half, filter_row, 0)
        mixed = jnp.dot(product[:lines], mix_ref[...], preferred_element_type=jnp.float32)
        here = x_ref[pl.ds(start, half)].reshape(lines, channels)
        latent = here.astype(jnp.float32) + mixed
        mean = jnp.mean(latent, axis=1, keepdims=True)
        centred = latent - mean
        variance = jnp.mean(centred * centred, axis=1, keepdims=True)
        normed = (centred * lax.rsqrt(variance + norm_eps) * gain_ref[...][None, :]).astype(jnp.bfloat16)
        raised = jnp.dot(normed, up_ref[...], preferred_element_type=jnp.float32)
        hidden = 0.5 * raised * (1.0 + lax.erf(raised * math.sqrt(0.5)))
        lowered = jnp.dot(
            hidden.astype(jnp.bfloat16), down_ref[...], preferred_element_type=jnp.float32
        )
        result = (latent + lowered).astype(jnp.bfloat16)
        out_ref[pl.ds(start, half)] = result.reshape(half, cols, channels)

    puts = []
    for stage, (low, high) in zip(copies, groups):
        each(stage, False, lambda copy: copy.wait_recv())
        if stage is copies[0]:
            for load in loads:
                load.wait()
        group(low, high)
        part = pl.ds(jnp.where(north, low, rows - high), high - low)
        put = pltpu.make_async_copy(out_ref.at[part], out_hbm.at[part], out_sem.at[len(puts)])
        put.start()
        puts.append(put)
    for stage in copies:
        each(stage, True, lambda copy: copy.wait_send())
    for put in puts:
        put.wait()


def on_device(
    lon_count,
    lat_count,
    fields,
    support_rows,
    support_lons,
    support_weights,
    mix_weight,
    norm_gain,
    up_weight,
    down_weight,
):
    channels, rows, cols = fields.shape
    bases, hidden = mix_weight.shape[0], up_weight.shape[1]
    lon_total = lon_count * cols
    plan = plan_copies(lon_count, lat_count, rows, cols)
    count = sum(len(stage) for stage in plan[1])
    in_vmem = pl.BlockSpec(memory_space=pltpu.VMEM)
    anywhere = pl.BlockSpec(memory_space=pl.ANY)
    result = pl.pallas_call(
        functools.partial(block_kernel, lon_count, lat_count, plan),
        out_shape=jax.ShapeDtypeStruct((rows, cols, channels), jnp.bfloat16),
        in_specs=[anywhere] + [in_vmem] * 4 + [anywhere] * 3,
        out_specs=anywhere,
        scratch_shapes=[
            pltpu.VMEM((rows, cols, channels), jnp.bfloat16),
            pltpu.VMEM((rows, cols, channels), jnp.bfloat16),
            pltpu.VMEM((rows + 2, lon_total, channels), jnp.bfloat16),
            pltpu.VMEM((rows, bases * cols, 3 * lon_total), jnp.bfloat16),
            pltpu.VMEM((rows // 2 * cols, bases * channels), jnp.bfloat16),
            pltpu.VMEM((bases * channels, channels), jnp.bfloat16),
            pltpu.VMEM((channels, hidden), jnp.bfloat16),
            pltpu.VMEM((hidden, channels), jnp.bfloat16),
            pltpu.SemaphoreType.DMA((count,)),
            pltpu.SemaphoreType.DMA((count,)),
            pltpu.SemaphoreType.DMA((4,)),
            pltpu.SemaphoreType.DMA((len(plan[0]),)),
        ],
        compiler_params=pltpu.CompilerParams(
            collective_id=0, has_side_effects=True, vmem_limit_bytes=56 * 1024 * 1024
        ),
    )(
        jnp.transpose(fields, (1, 2, 0)),
        jnp.transpose(support_rows, (0, 2, 1)),
        jnp.transpose(support_lons, (0, 2, 1)),
        jnp.transpose(support_weights, (0, 2, 1)),
        norm_gain,
        mix_weight.reshape(bases * channels, channels),
        up_weight,
        down_weight,
    )
    return jnp.transpose(result, (2, 0, 1))


def solution(mesh):
    in_specs = (P("member", "lat", "lon"), P(), P(), P(), P(), P(), P(), P())
    out_specs = P("member", "lat", "lon")
    return jax.shard_map(
        functools.partial(on_device, mesh.shape["lon"], mesh.shape["lat"]),
        mesh=mesh,
        in_specs=in_specs,
        out_specs=out_specs,
        check_vma=False,
    )
```
